256 devices in a mesh: freq: 4 (over y), mx: 8 (over x, core), my: 8 (over z).
Axes of the slice: x: 4, y: 4, z: 8, core: 2. Of those that a mesh axis runs over, the one named last changes fastest.
Arguments:
- adjoint_rhs: float32 [4, 2, 3, 512, 2048], P('freq', None, None, 'mx', 'my'), may hold values from -4 to 6
- state: bfloat16 [4, 2, 3, 512, 2048], P('freq', None, None, 'mx', 'my'), may hold values from -1.5 to 1.5
- density: float32 [512, 2048], P('mx', 'my'), may hold values from 0.85 to 1
- stiffness: float32 [512, 2048], P('mx', 'my'), may hold values from 1.5 to 4
- mass: float32 [512, 2048], P('mx', 'my'), may hold values from 0.2 to 1
- omega: float32 [4], P('freq'), may hold values from 0.15 to 0.45
- send_rows: int32 [64, 2048], P(('mx', 'my')), may hold values from 0 to 16383, as said below
- recv_rows: int32 [64, 2048], P(('mx', 'my')), may hold values from 0 to 16383, as said below
- mortar_weight: float32 [64, 2048], P(('mx', 'my')), may hold values from 0 to 1.5, as said below
Outputs:
- adjoint: float32 [4, 2, 3, 512, 2048], P('freq', None, None, 'mx', 'my')
- filtered_sensitivity: float32 [512, 2048], P('mx', 'my')
The draws below stay inside these ranges and needn't reach their ends.
Inputs may be any that keep to these rules, and one draw needn't show every extreme that they name: `send_rows`: a local cell of the sending device; slots past the live count of a device pair hold 0. `recv_rows`: a local cell of the receiving device; empty slots hold 0. Live slots of a pair come first, up to 32 of them. `mortar_weight`: zero exactly in empty slots, at least 0.5 in live ones; every receiving device has a source device with all 32 slots live.
All inputs are finite; a program needn't handle non-finite values.
Results may differ from the reference program's by a relative error of at most 0.0003.
Values may be sent and summed in bfloat16 or wider, within the bound.
A program may use at most 64 MiB of HBM per device.

```python
import math
import jax
import jax.numpy as jnp

CX = 64
CY = 256
CAP = 32
ITERS = 20
FREQS = 4
PEERS = 64
CELLS_DEV = 16384
NX = 512
NY = 2048
N_MX = 8
N_MY = 8


def live_slots(key):
    counts = jax.random.randint(jax.random.fold_in(key, 11), (PEERS, PEERS), CAP // 2, CAP + 1)
    forced = (jnp.arange(PEERS) * 7 + 3) % PEERS
    counts = jnp.where(jnp.arange(PEERS)[None, :] == forced[:, None], CAP, counts)
    return jnp.arange(CAP)[None, None, :] < counts[:, :, None]


def draw_recv_rows(key, part):
    live = live_slots(key)
    rows = jax.random.randint(jax.random.fold_in(key, 12), (PEERS, PEERS, CAP), 0, CELLS_DEV)
    return jnp.where(live, rows, 0).astype(jnp.int32).reshape(PEERS, PEERS * CAP)


def draw_send_rows(key, part):
    live = jnp.transpose(live_slots(key), (1, 0, 2))
    rows = jax.random.randint(jax.random.fold_in(key, 13), (PEERS, PEERS, CAP), 0, CELLS_DEV)
    return jnp.where(live, rows, 0).astype(jnp.int32).reshape(PEERS, PEERS * CAP)


def draw_mortar_weight(key, part):
    live = live_slots(key)
    values = jax.random.uniform(jax.random.fold_in(key, 14), (PEERS, PEERS, CAP), jnp.float32, 0.5, 1.5)
    return jnp.where(live, values, 0.0).astype(jnp.float32).reshape(PEERS, PEERS * CAP)


def draw_adjoint_rhs(key, part):
    shape = (FREQS, 2, 3, NX, NY)
    xs = (jnp.arange(NX, dtype=jnp.float32) + 0.5) / NX
    ys = (jnp.arange(NY, dtype=jnp.float32) + 0.5) / NY
    phase_x = jax.random.uniform(jax.random.fold_in(key, 21), (FREQS, 2, 3, 1, 1), jnp.float32, 0.0, 2.0 * math.pi)
    phase_y = jax.random.uniform(jax.random.fold_in(key, 22), (FREQS, 2, 3, 1, 1), jnp.float32, 0.0, 2.0 * math.pi)
    amp = jax.random.uniform(jax.random.fold_in(key, 23), (FREQS, 2, 3, 1, 1), jnp.float32, 0.8, 1.4)
    rough = jnp.clip(jax.random.normal(jax.random.fold_in(key, 24), shape, jnp.float32), -4.0, 4.0)
    wave = jnp.sin(2.0 * math.pi * xs[:, None] + phase_x) * jnp.sin(2.0 * math.pi * ys[None, :] + phase_y)
    smooth = amp * (1.0 + 0.4 * wave)
    return (smooth + rough).astype(jnp.float32)


def block_levels(rng, shape, shards, low, top_value):
    level = 1.0
    for dim, parts in shards:
        heights = jax.random.uniform(jax.random.fold_in(jax.random.fold_in(rng, 6), dim), (parts,), jnp.float32, low / len(shards), top_value / len(shards))
        level = level * jnp.repeat(jnp.exp(heights), shape[dim] // parts).reshape((-1,) + (1,) * (len(shape) - 1 - dim))
    return level


def centred(key, dims, width, reach, pieces=(), held_as=jnp.bfloat16):
    values = width * jax.random.normal(key, dims, jnp.float32)
    if pieces:
        values = values * block_levels(key, dims, pieces, -0.22, 0.18)
    return jnp.clip(values, -reach, reach).astype(held_as)


def setup_inputs(seed: int = 0) -> dict:
    keys = jax.random.split(jax.random.key(seed), 10)
    adjoint_rhs = draw_adjoint_rhs(jax.random.fold_in(keys[9], 71), 0)
    state = centred(keys[1], (FREQS, 2, 3, NX, NY), 0.1, 1.5, ((0, 4), (3, 8), (4, 8)))
    density = jnp.clip(jnp.exp(math.log(1.0) - 0.1625189 * jax.random.uniform(keys[2], (NX, NY), jnp.float32) ** block_levels(keys[2], (NX, NY), ((0, 8), (1, 8)), -0.2, 0.2)), 0.85, 1.0)
    stiffness = jnp.clip(jnp.exp(math.log(4.0) - 0.98082925 * jax.random.uniform(keys[3], (NX, NY), jnp.float32) ** block_levels(keys[3], (NX, NY), ((0, 8), (1, 8)), -0.2, 0.2)), 1.5, 4.0)
    mass = jnp.clip(0.2 + 0.8 * jax.random.uniform(keys[4], (NX, NY), jnp.float32) ** block_levels(keys[4], (NX, NY), ((0, 8), (1, 8)), -0.2, 0.2), 0.2, 1.0)
    omega = jnp.clip(jnp.exp(math.log(0.45) - 1.0986122 * jax.random.uniform(keys[5], (FREQS,), jnp.float32) ** block_levels(keys[5], (FREQS,), ((0, 4),), -0.2, 0.2)), 0.15, 0.45)
    send_rows = draw_send_rows(jax.random.fold_in(keys[9], 71), 0)
    recv_rows = draw_recv_rows(jax.random.fold_in(keys[9], 71), 0)
    mortar_weight = draw_mortar_weight(jax.random.fold_in(keys[9], 71), 0)
    return dict(adjoint_rhs=adjoint_rhs, state=state, density=density, stiffness=stiffness, mass=mass, omega=omega, send_rows=send_rows, recv_rows=recv_rows, mortar_weight=mortar_weight)


def edge_sum(field):
    padded = jnp.pad(field, ((0, 0), (1, 1), (1, 1)))
    return padded[:, 2:, 1:-1] + padded[:, :-2, 1:-1] + padded[:, 1:-1, 2:] + padded[:, 1:-1, :-2]


def global_cells(device, local):
    row_dev = device // N_MY
    col_dev = device % N_MY
    return (row_dev * CX + local // CY) * NY + col_dev * CY + local % CY


def reference(adjoint_rhs, state, density, stiffness, mass, omega, send_rows, recv_rows, mortar_weight):
    peers = N_MX * N_MY
    senders = send_rows.reshape(peers, peers, CAP).transpose(1, 0, 2)
    dest_ids = jnp.arange(peers, dtype=jnp.int32)[:, None, None]
    src_ids = jnp.arange(peers, dtype=jnp.int32)[None, :, None]
    sources = global_cells(src_ids, senders).reshape(-1)
    targets = global_cells(dest_ids, recv_rows.reshape(peers, peers, CAP)).reshape(-1)
    weights = mortar_weight.reshape(-1)
    stiff = density ** 3 * stiffness
    dstiff = 3.0 * density ** 2 * stiffness
    rmass = density * mass
    mdiag = jnp.zeros((NX * NY,), jnp.float32).at[targets].add(weights).reshape(NX, NY)
    adjoints = []
    total = jnp.zeros((NX, NY), jnp.float32)
    for freq_index in range(FREQS):
        w = omega[freq_index]
        real_d = 4.4 * stiff + 0.3 + mdiag - w * w * rmass
        imag_d = 0.2 * w * (stiff + rmass)
        den = real_d * real_d + imag_d * imag_d
        rhs = adjoint_rhs[freq_index].reshape(6, NX, NY)

        def sweep(step, field):
            flat = field.reshape(6, NX * NY)
            mortar = jnp.zeros((6, NX * NY), jnp.float32).at[:, targets].add(flat[:, sources] * weights)
            h = rhs + stiff * edge_sum(field) + mortar.reshape(6, NX, NY)
            new_re = (h[:3] * real_d + h[3:] * imag_d) / den
            new_im = (h[3:] * real_d - h[:3] * imag_d) / den
            return jnp.concatenate([new_re, new_im], axis=0)

        field = jax.lax.fori_loop(0, ITERS, sweep, jnp.zeros((6, NX, NY), jnp.float32))
        adjoints.append(field.reshape(2, 3, NX, NY))
        u = state[freq_index].reshape(6, NX, NY).astype(jnp.float32)
        nb = edge_sum(u)
        da = 4.4 * dstiff - w * w * mass
        db = 0.2 * w * (dstiff + mass)
        t_re = da * u[:3] - db * u[3:] - dstiff * nb[:3]
        t_im = da * u[3:] + db * u[:3] - dstiff * nb[3:]
        total = total - jnp.sum(field[:3] * t_re - field[3:] * t_im, axis=0)
    weighted = jnp.pad(density * total, 1)
    filt = weighted[1:-1, 1:-1]
    filt = filt + 0.5 * (weighted[2:, 1:-1] + weighted[:-2, 1:-1] + weighted[1:-1, 2:] + weighted[1:-1, :-2])
    filt = filt + 0.25 * (weighted[2:, 2:] + weighted[:-2, :-2] + weighted[2:, :-2] + weighted[:-2, 2:])
    return jnp.stack(adjoints, axis=0), filt / (4.0 * density)
```

```python
import functools

import jax
import jax.numpy as jnp
from jax import lax
from jax.experimental import pallas as pl
from jax.experimental.pallas import tpu as pltpu
from jax.sharding import PartitionSpec as P

ITERS = 20
MESH = pl.DeviceIdType.MESH
F32 = jnp.float32
BF16 = jnp.bfloat16


def onehot(a, b):
    return jnp.where(a == b, 1.0, 0.0).astype(F32)


def sweeps_kernel(
    n_mx,
    n_my,
    rhs_ref,
    dens_ref,
    stiffness_ref,
    mass_ref,
    omega_ref,
    send_ref,
    recv_ref,
    weight_ref,
    out_ref,
    field,
    field_b,
    stiff_s,
    gain_p,
    gain_q,
    pick_y,
    pick_x,
    put_y,
    put_x,
    wrow,
    spread,
    msg_out,
    msg_in,
    y_out,
    y_in,
    x_out,
    x_in,
    msg_send_sem,
    msg_recv_sem,
    own_sem,
    halo_send_sem,
    halo_recv_sem,
):
    i = lax.axis_index("mx")
    j = lax.axis_index("my")
    peers = n_mx * n_my
    me = i * n_my + j
    rx, ry = dens_ref.shape
    slots = send_ref.shape[1]
    tiles = slots // 128

    def at(di, dj):
        return {
            "mx": lax.rem(i + di + n_mx, n_mx),
            "my": lax.rem(j + dj + n_my, n_my),
        }

    offsets = [(a, b) for a in range(n_mx) for b in range(n_my) if a or b]

    def far(o):
        a, b = o
        return -(min(b, n_my - b) + min(a, n_mx - a) / 2.0)

    offsets.sort(key=far)

    barrier = pltpu.get_barrier_semaphore()
    for a, b in offsets:
        pl.semaphore_signal(barrier, inc=1, device_id=at(a, b), device_id_type=MESH)

    w = omega_ref[0]
    dens = dens_ref[...]
    mass = mass_ref[...]
    stiff = dens * dens * dens * stiffness_ref[...]
    rmass = dens * mass
    stiff_s[...] = stiff

    lane = lax.broadcasted_iota(jnp.int32, (8, 128), 1)
    sub = lax.broadcasted_iota(jnp.int32, (8, 128), 0)
    block = lax.shift_right_logical(lane, 5)
    comp = lax.bitwise_and(sub, 3)
    here = block == comp

    sub_y = lax.broadcasted_iota(jnp.int32, (ry, 128), 0)
    sub_x = lax.broadcasted_iota(jnp.int32, (rx, 128), 0)
    lane_y = lax.broadcasted_iota(jnp.int32, (128, ry), 1)
    lane_row = lax.broadcasted_iota(jnp.int32, (1, 128), 1)
    low = lane_row < rx
    for t in range(tiles + 1):
        cols = slice(t * 128, (t + 1) * 128)
        if t < tiles:
            src = send_ref[:, cols]
            dst = recv_ref[:, cols]
            sx, sy = lax.shift_right_logical(src, 8), lax.bitwise_and(src, ry - 1)
            dx, dy = lax.shift_right_logical(dst, 8), lax.bitwise_and(dst, ry - 1)
        else:
            sx = dx = jnp.where(low, lane_row, lane_row - rx)
            sy = jnp.where(low, 0, ry - 1)
            dy = jnp.where(low, ry - 1, 0)
        pick_y[:, cols] = onehot(sub_y, sy).astype(BF16)
        pick_x[:, cols] = onehot(sub_x, sx)
        put_x[:, cols] = onehot(sub_x, dx).astype(BF16)
        turned = jnp.broadcast_to(dy.astype(F32), (128, 128)).T.astype(jnp.int32)
        put_y[cols, :] = onehot(lane_y, jnp.concatenate([turned] * (ry // 128), axis=1)).astype(BF16)
    wrow[:, :slots] = weight_ref[...]
    eye_low = onehot(sub_x, lane_row)
    eye_high = onehot(sub_x, lane_row - rx)
    wrow[:, slots:] = jnp.sum(
        stiff[:, ry - 1 :] * eye_low + stiff[:, :1] * eye_high, axis=0, keepdims=True
    )

    whole = weight_ref[...]
    hi = whole.astype(BF16)
    rest = whole - hi.astype(F32)
    mid = rest.astype(BF16)
    lo = (rest - mid.astype(F32)).astype(BF16)
    mdiag = jnp.zeros((rx, ry), F32)
    for piece in (hi, mid, lo):
        spread[0:rx, :slots] = put_x[:, :slots] * jnp.broadcast_to(piece, (rx, slots))
        mdiag += jnp.dot(spread[0:rx, :slots], put_y[:slots, :], preferred_element_type=F32)

    real_d = 4.4 * stiff + 0.3 + mdiag - w * w * rmass
    imag_d = 0.2 * w * (stiff + rmass)
    den = real_d * real_d + imag_d * imag_d
    gain_p[...] = real_d / den
    gain_q[...] = imag_d / den

    def update(h):
        p, q = gain_p[...], gain_q[...]
        for c in range(3):
            re, im = h(c), h(c + 3)
            new_re = re * p + im * q
            new_im = im * p - re * q
            for k, v in ((c, new_re), (c + 3, new_im)):
                field[k, :, :] = v
                field_b[k * rx : (k + 1) * rx, :] = v.astype(BF16)

    update(lambda c: rhs_ref[c])

    pl.semaphore_wait(barrier, peers - 1)

    up_ok = jnp.where(i > 0, 1.0, 0.0).astype(F32)
    down_ok = jnp.where(i < n_mx - 1, 1.0, 0.0).astype(F32)
    left_ok = jnp.where(j > 0, 1.0, 0.0).astype(F32)
    right_ok = jnp.where(j < n_my - 1, 1.0, 0.0).astype(F32)
    zero_row = jnp.zeros((1, 128), F32)

    def pick(cols, width):
        g = jnp.dot(field_b[...], pick_y[:, cols], preferred_element_type=F32)
        mask = pick_x[:, cols]
        rows = [
            jnp.sum(g[c * rx : (c + 1) * rx] * mask, axis=0, keepdims=True) for c in range(6)
        ]
        zero = jnp.zeros((1, width), F32)
        return jnp.concatenate(rows[:3] + [zero] + rows[3:] + [zero], axis=0)

    def remote(src, dst, ssem, rsem, to):
        return pltpu.make_async_remote_copy(
            src_ref=src, dst_ref=dst, send_sem=ssem, recv_sem=rsem, device_id=to, device_id_type=MESH
        )

    def sweep(step, carry):
        par = lax.rem(step, 2)

        for c in range(6):
            x_out[0, c : c + 1, :] = field[c, 0:1, :]
            x_out[1, c : c + 1, :] = field[c, rx - 1 : rx, :]
        halo = halo_recv_sem.at[par]
        remote(x_out.at[0], x_in.at[par, 1], halo_send_sem.at[0], halo.at[1], at(-1, 0)).start()
        remote(x_out.at[1], x_in.at[par, 0], halo_send_sem.at[1], halo.at[0], at(1, 0)).start()

        for t in range(tiles // 2):
            rows = pick(slice(t * 256, (t + 1) * 256), 256)
            for half in range(2):
                r = rows[:, half * 128 : (half + 1) * 128]
                x = jnp.where(
                    comp == 1, pltpu.roll(r, 32, 1), jnp.where(comp == 2, pltpu.roll(r, 64, 1), r)
                )
                for d in range(4):
                    y = x if d == 0 else pltpu.roll(x, 128 - 32 * d, 1)
                    z = jnp.where(here, y, 0.0)
                    m = jnp.concatenate(
                        [
                            jnp.sum(z[:4], axis=0, keepdims=True),
                            jnp.sum(z[4:], axis=0, keepdims=True),
                        ],
                        axis=0,
                    )
                    msg_out[(2 * t + half) * 4 + d] = m.astype(BF16)
        own = pltpu.make_async_copy(msg_out.at[me], msg_in.at[par, me], own_sem)
        own.start()
        for a, b in offsets:
            to = at(a, b)
            remote(
                msg_out.at[to["mx"] * n_my + to["my"]],
                msg_in.at[par, me],
                msg_send_sem,
                msg_recv_sem.at[par],
                to,
            ).start()

        y_out[...] = pick(slice(slots, slots + 128), 128)
        remote(y_out, y_in.at[par, 1], halo_send_sem.at[2], halo.at[3], at(0, -1)).start()
        remote(y_out, y_in.at[par, 0], halo_send_sem.at[3], halo.at[2], at(0, 1)).start()

        for side in range(2):
            pltpu.make_async_copy(x_in.at[par, side], x_in.at[par, side], halo.at[side]).wait()
            pltpu.make_async_copy(y_in.at[par, side], y_in.at[par, side], halo.at[2 + side]).wait()
        own.wait()
        most = pl.ds(0, peers - 1)
        pltpu.make_async_copy(
            msg_in.at[par, most], msg_in.at[par, most], msg_recv_sem.at[par]
        ).wait()

        for t in range(tiles + 1):
            cols = slice(t * 128, (t + 1) * 128)
            if t < tiles:
                got = None
                for d in range(4):
                    m = msg_in[par, 4 * t + d].astype(F32)
                    u = jnp.concatenate(
                        [
                            jnp.broadcast_to(m[0:1], (4, 128)),
                            jnp.broadcast_to(m[1:2], (4, 128)),
                        ],
                        axis=0,
                    )
                    u = jnp.where(here, u, 0.0)
                    if d:
                        u = pltpu.roll(u, 32 * d, 1)
                    got = u if got is None else got + u
                got = jnp.where(
                    comp == 1,
                    pltpu.roll(got, 96, 1),
                    jnp.where(comp == 2, pltpu.roll(got, 64, 1), got),
                )
            else:
                got = jnp.where(
                    lane < rx, y_in[par, 1] * right_ok, y_in[par, 0] * left_ok
                )
            got = got * wrow[:, cols]
            mask = put_x[:, cols]
            for c in range(6):
                r = c + c // 3
                spread[c * rx : (c + 1) * rx, cols] = mask * jnp.broadcast_to(
                    got[r : r + 1].astype(BF16), (rx, 128)
                )
        coupled = jnp.dot(spread[...], put_y[...], preferred_element_type=F32)

        pltpu.make_async_copy(msg_out.at[most], msg_out.at[most], msg_send_sem).wait()
        for side in range(2):
            pltpu.make_async_copy(x_out.at[side], x_out.at[side], halo_send_sem.at[side]).wait()
            pltpu.make_async_copy(y_out, y_out, halo_send_sem.at[2 + side]).wait()

        st = stiff_s[...]
        lane_w = lax.broadcasted_iota(jnp.int32, (rx, ry), 1)
        sub_w = lax.broadcasted_iota(jnp.int32, (rx, ry), 0)

        def h(c):
            f = field[c]
            above = jnp.broadcast_to(x_in[par, 0, c : c + 1, :] * up_ok, (rx, ry))
            below = jnp.broadcast_to(x_in[par, 1, c : c + 1, :] * down_ok, (rx, ry))
            nb = jnp.where(sub_w == 0, above, pltpu.roll(f, 1, 0))
            nb += jnp.where(sub_w == rx - 1, below, pltpu.roll(f, rx - 1, 0))
            nb += jnp.where(lane_w == 0, 0.0, pltpu.roll(f, 1, 1))
            nb += jnp.where(lane_w == ry - 1, 0.0, pltpu.roll(f, ry - 1, 1))
            return rhs_ref[c] + st * nb + coupled[c * rx : (c + 1) * rx]

        update(h)
        return carry

    lax.fori_loop(1, ITERS, sweep, 0)
    out_ref[...] = field[...]


def solve(n_mx, n_my, rhs, density, stiffness, mass, omega, send_rows, recv_rows, mortar_weight):
    rx, ry = density.shape
    slots = send_rows.shape[1]
    wide = slots + 128
    peers = n_mx * n_my
    vmem = pl.BlockSpec(memory_space=pltpu.VMEM)
    return pl.pallas_call(
        functools.partial(sweeps_kernel, n_mx, n_my),
        out_shape=jax.ShapeDtypeStruct((6, rx, ry), F32),
        in_specs=[vmem] * 4 + [pl.BlockSpec(memory_space=pltpu.SMEM)] + [vmem] * 3,
        out_specs=vmem,
        scratch_shapes=[
            pltpu.VMEM((6, rx, ry), F32),
            pltpu.VMEM((6 * rx, ry), BF16),
            pltpu.VMEM((rx, ry), F32),
            pltpu.VMEM((rx, ry), F32),
            pltpu.VMEM((rx, ry), F32),
            pltpu.VMEM((ry, wide), BF16),
            pltpu.VMEM((rx, wide), F32),
            pltpu.VMEM((wide, ry), BF16),
            pltpu.VMEM((rx, wide), BF16),
            pltpu.VMEM((1, wide), F32),
            pltpu.VMEM((6 * rx, wide), BF16),
            pltpu.VMEM((peers, 2, 128), BF16),
            pltpu.VMEM((2, peers, 2, 128), BF16),
            pltpu.VMEM((8, 128), F32),
            pltpu.VMEM((2, 2, 8, 128), F32),
            pltpu.VMEM((2, 8, ry), F32),
            pltpu.VMEM((2, 2, 8, ry), F32),
            pltpu.SemaphoreType.DMA,
            pltpu.SemaphoreType.DMA((2,)),
            pltpu.SemaphoreType.DMA,
            pltpu.SemaphoreType.DMA((4,)),
            pltpu.SemaphoreType.DMA((2, 4)),
        ],
        compiler_params=pltpu.CompilerParams(collective_id=0, has_side_effects=True),
    )(rhs, density, stiffness, mass, omega, send_rows, recv_rows, mortar_weight)


def extended(x, sides, width):
    for axis, dim in sides:
        size, length = (lax.axis_size(axis), x.shape[dim])
        up = [(i, (i + 1) % size) for i in range(size - 1)]
        down = [(j, i) for i, j in up]
        last = lax.slice_in_dim(x, length - width, length, axis=dim)
        first = lax.slice_in_dim(x, 0, width, axis=dim)
        before = lax.ppermute(last, axis, up)
        after = lax.ppermute(first, axis, down)
        x = jnp.concatenate([before, x, after], axis=dim)
    return x


def on_device(
    adjoint_rhs, state, density, stiffness, mass, omega, send_rows, recv_rows, mortar_weight
):
    rows_x, rows_y = density.shape
    w = omega[0]
    dstiff = 3.0 * density**2 * stiffness
    rhs = adjoint_rhs.reshape(6, rows_x, rows_y)
    field = solve(
        lax.axis_size("mx"), lax.axis_size("my"),
        rhs, density, stiffness, mass, omega, send_rows, recv_rows, mortar_weight,
    )
    state_six = state.reshape(6, rows_x, rows_y)
    state_pad = extended(state_six, (("mx", 1), ("my", 2)), 1).astype(jnp.float32)
    u = state_six.astype(jnp.float32)
    nb = (
        state_pad[:, 2:, 1:-1]
        + state_pad[:, :-2, 1:-1]
        + state_pad[:, 1:-1, 2:]
        + state_pad[:, 1:-1, :-2]
    )
    da = 4.4 * dstiff - w * w * mass
    db = 0.2 * w * (dstiff + mass)
    t_re = da * u[:3] - db * u[3:] - dstiff * nb[:3]
    t_im = da * u[3:] + db * u[:3] - dstiff * nb[3:]
    sens = -jnp.sum(field[:3] * t_re - field[3:] * t_im, axis=0)
    total = lax.psum(sens, "freq")
    weighted = extended(density * total, (("mx", 0), ("my", 1)), 1)
    filt = weighted[1:-1, 1:-1]
    filt = filt + 0.5 * (
        weighted[2:, 1:-1] + weighted[:-2, 1:-1] + weighted[1:-1, 2:] + weighted[1:-1, :-2]
    )
    filt = filt + 0.25 * (
        weighted[2:, 2:] + weighted[:-2, :-2] + weighted[2:, :-2] + weighted[:-2, 2:]
    )
    return (field.reshape(1, 2, 3, rows_x, rows_y), filt / (4.0 * density))


def solution(mesh):
    return jax.shard_map(
        on_device,
        mesh=mesh,
        in_specs=(
            P("freq", None, None, "mx", "my"),
            P("freq", None, None, "mx", "my"),
            P("mx", "my"),
            P("mx", "my"),
            P("mx", "my"),
            P("freq"),
            P(("mx", "my"), None),
            P(("mx", "my"), None),
            P(("mx", "my"), None),
        ),
        out_specs=(P("freq", None, None, "mx", "my"), P("mx", "my")),
        check_vma=False,
    )
```

```python
import functools

import jax
import jax.numpy as jnp
from jax import lax
from jax.experimental import pallas as pl
from jax.experimental.pallas import tpu as pltpu
from jax.sharding import PartitionSpec as P

ITERS = 20
MESH = pl.DeviceIdType.MESH
F32 = jnp.float32
BF16 = jnp.bfloat16


def onehot(a, b):
    return jnp.where(a == b, 1.0, 0.0).astype(F32)


def sweeps_kernel(
    n_freq,
    n_mx,
    n_my,
    rhs_ref,
    state_ref,
    dens_ref,
    stiffness_ref,
    mass_ref,
    omega_ref,
    send_ref,
    recv_ref,
    weight_ref,
    out_ref,
    filt_ref,
    field,
    field_b,
    field_l,
    stiff_s,
    gain_p,
    gain_q,
    pick_y,
    pick_x,
    put_y,
    put_x,
    wrow,
    spread,
    msg_out,
    msg_in,
    y_out,
    y_in,
    x_out,
    x_in,
    msg_send_sem,
    msg_recv_sem,
    own_sem,
    halo_send_sem,
    halo_recv_sem,
    tangent,
    sx_out,
    sx_in,
    sy_out,
    sy_in,
    state_send_sem,
    state_recv_sem,
    sens_out,
    sens_in,
    edge_out,
    edge_in,
    sens_send_sem,
    sens_recv_sem,
    edge_send_sem,
    edge_recv_sem,
):
    fr = lax.axis_index("freq")
    i = lax.axis_index("mx")
    j = lax.axis_index("my")
    peers = n_mx * n_my
    me = i * n_my + j
    rx, ry = dens_ref.shape
    slots = send_ref.shape[1]
    tiles = slots // 128

    def at(di, dj, df=0):
        return {
            "freq": lax.rem(fr + df, n_freq),
            "mx": lax.rem(i + di + n_mx, n_mx),
            "my": lax.rem(j + dj + n_my, n_my),
        }

    offsets = [(a, b) for a in range(n_mx) for b in range(n_my) if a or b]

    def far(o):
        a, b = o
        return -(min(b, n_my - b) + min(a, n_mx - a) / 2.0)

    offsets.sort(key=far)

    barrier = pltpu.get_barrier_semaphore()
    for a, b in offsets:
        pl.semaphore_signal(barrier, inc=1, device_id=at(a, b), device_id_type=MESH)
    around = [(a, b) for a in (-1, 0, 1) for b in (-1, 0, 1)]
    for df in range(1, n_freq):
        for a, b in around:
            pl.semaphore_signal(barrier, inc=1, device_id=at(a, b, df), device_id_type=MESH)

    w = omega_ref[0]
    dens = dens_ref[...]
    mass = mass_ref[...]
    stiff = dens * dens * dens * stiffness_ref[...]
    rmass = dens * mass
    stiff_s[...] = stiff

    lane = lax.broadcasted_iota(jnp.int32, (8, 128), 1)
    sub = lax.broadcasted_iota(jnp.int32, (8, 128), 0)
    block = lax.shift_right_logical(lane, 5)
    comp = lax.bitwise_and(sub, 3)
    here = block == comp

    sub_y = lax.broadcasted_iota(jnp.int32, (ry, 128), 0)
    sub_x = lax.broadcasted_iota(jnp.int32, (rx, 128), 0)
    lane_y = lax.broadcasted_iota(jnp.int32, (128, ry), 1)
    lane_row = lax.broadcasted_iota(jnp.int32, (1, 128), 1)
    low = lane_row < rx
    for t in range(tiles + 1):
        cols = slice(t * 128, (t + 1) * 128)
        if t < tiles:
            src = send_ref[:, cols]
            dst = recv_ref[:, cols]
            sx, sy = lax.shift_right_logical(src, 8), lax.bitwise_and(src, ry - 1)
            dx, dy = lax.shift_right_logical(dst, 8), lax.bitwise_and(dst, ry - 1)
        else:
            sx = dx = jnp.where(low, lane_row, lane_row - rx)
            sy = jnp.where(low, 0, ry - 1)
            dy = jnp.where(low, ry - 1, 0)
        pick_y[:, cols] = onehot(sub_y, sy).astype(BF16)
        pick_x[:, cols] = onehot(sub_x, sx)
        put_x[:, cols] = onehot(sub_x, dx).astype(BF16)
        turned = jnp.broadcast_to(dy.astype(F32), (128, 128)).T.astype(jnp.int32)
        put_y[cols, :] = onehot(lane_y, jnp.concatenate([turned] * (ry // 128), axis=1)).astype(BF16)
    put_y[slots + 128 :, :] = put_y[slots : slots + 128, :]
    wrow[:, :slots] = weight_ref[...]
    eye_low = onehot(sub_x, lane_row)
    eye_high = onehot(sub_x, lane_row - rx)
    wrow[:, slots:] = jnp.sum(
        stiff[:, ry - 1 :] * eye_low + stiff[:, :1] * eye_high, axis=0, keepdims=True
    )

    whole = weight_ref[...]
    hi = whole.astype(BF16)
    rest = whole - hi.astype(F32)
    mid = rest.astype(BF16)
    lo = (rest - mid.astype(F32)).astype(BF16)
    mdiag = jnp.zeros((rx, ry), F32)
    for piece in (hi, mid, lo):
        spread[0:rx, :slots] = put_x[:, :slots] * jnp.broadcast_to(piece, (rx, slots))
        mdiag += jnp.dot(spread[0:rx, :slots], put_y[:slots, :], preferred_element_type=F32)

    real_d = 4.4 * stiff + 0.3 + mdiag - w * w * rmass
    imag_d = 0.2 * w * (stiff + rmass)
    den = real_d * real_d + imag_d * imag_d
    gain_p[...] = real_d / den
    gain_q[...] = imag_d / den

    def update(h):
        p, q = gain_p[...], gain_q[...]
        for c in range(3):
            re, im = h(c), h(c + 3)
            new_re = re * p + im * q
            new_im = im * p - re * q
            for k, v in ((c, new_re), (c + 3, new_im)):
                field[k, :, :] = v
                high = v.astype(BF16)
                field_b[k * rx : (k + 1) * rx, :] = high
                field_l[k * rx : (k + 1) * rx, :] = (v - high.astype(F32)).astype(BF16)

    update(lambda c: rhs_ref[c])

    pl.semaphore_wait(barrier, peers - 1 + 9 * (n_freq - 1))

    up_ok = jnp.where(i > 0, 1.0, 0.0).astype(F32)
    down_ok = jnp.where(i < n_mx - 1, 1.0, 0.0).astype(F32)
    left_ok = jnp.where(j > 0, 1.0, 0.0).astype(F32)
    right_ok = jnp.where(j < n_my - 1, 1.0, 0.0).astype(F32)
    zero_row = jnp.zeros((1, 128), F32)

    def pick(cols, width, source):
        g = jnp.dot(source, pick_y[:, cols], preferred_element_type=F32)
        mask = pick_x[:, cols]
        rows = [
            jnp.sum(g[c * rx : (c + 1) * rx] * mask, axis=0, keepdims=True) for c in range(6)
        ]
        zero = jnp.zeros((1, width), F32)
        return jnp.concatenate(rows[:3] + [zero] + rows[3:] + [zero], axis=0)

    def remote(src, dst, ssem, rsem, to):
        return pltpu.make_async_remote_copy(
            src_ref=src, dst_ref=dst, send_sem=ssem, recv_sem=rsem, device_id=to, device_id_type=MESH
        )

    edge_cols = slice(slots, slots + 128)

    def scatter(got, start, mask):
        for c in range(6):
            r = c + c // 3
            spread[c * rx : (c + 1) * rx, start : start + 128] = mask * jnp.broadcast_to(
                got[r : r + 1].astype(BF16), (rx, 128)
            )

    lane_w = lax.broadcasted_iota(jnp.int32, (rx, ry), 1)
    sub_w = lax.broadcasted_iota(jnp.int32, (rx, ry), 0)

    def across_x(f, above, below):
        up = jnp.where(sub_w == 0, jnp.broadcast_to(above, (rx, ry)), pltpu.roll(f, 1, 0))
        down = jnp.where(
            sub_w == rx - 1, jnp.broadcast_to(below, (rx, ry)), pltpu.roll(f, rx - 1, 0)
        )
        return up + down

    def across_y(f, before, after):
        left = jnp.where(lane_w == 0, before, pltpu.roll(f, 1, 1))
        return left + jnp.where(lane_w == ry - 1, after, pltpu.roll(f, ry - 1, 1))

    for c in range(6):
        sx_out[0, c : c + 1, :] = state_ref[c, 0:1, :].astype(F32)
        sx_out[1, c : c + 1, :] = state_ref[c, rx - 1 : rx, :].astype(F32)
    sy_out[...] = pick(edge_cols, 128, state_ref[...].reshape(6 * rx, ry))
    state_copies = [
        remote(sx_out.at[0], sx_in.at[1], state_send_sem.at[0], state_recv_sem.at[1], at(-1, 0)),
        remote(sx_out.at[1], sx_in.at[0], state_send_sem.at[1], state_recv_sem.at[0], at(1, 0)),
        remote(sy_out, sy_in.at[1], state_send_sem.at[2], state_recv_sem.at[3], at(0, -1)),
        remote(sy_out, sy_in.at[0], state_send_sem.at[3], state_recv_sem.at[2], at(0, 1)),
    ]
    for copy in state_copies:
        copy.start()

    def tangents():
        for copy in state_copies:
            copy.wait()
        got = jnp.where(lane < rx, sy_in[1] * right_ok, sy_in[0] * left_ok)
        scatter(got, slots, put_x[:, edge_cols])
        sides = jnp.dot(spread[:, edge_cols], put_y[edge_cols, :], preferred_element_type=F32)
        d = dens_ref[...]
        dstiff = 3.0 * (d * d) * stiffness_ref[...]
        m = mass_ref[...]
        da = 4.4 * dstiff - w * w * m
        db = 0.2 * w * (dstiff + m)

        def beside(c):
            u = state_ref[c].astype(F32)
            nb = across_x(u, sx_in[0, c : c + 1, :] * up_ok, sx_in[1, c : c + 1, :] * down_ok)
            return u, nb + across_y(u, 0.0, 0.0) + sides[c * rx : (c + 1) * rx]

        for c in range(3):
            u_re, nb_re = beside(c)
            u_im, nb_im = beside(c + 3)
            tangent[c, :, :] = da * u_re - db * u_im - dstiff * nb_re
            tangent[c + 3, :, :] = da * u_im + db * u_re - dstiff * nb_im

    def sweep(step, carry):
        par = lax.rem(step, 2)

        for c in range(6):
            x_out[0, c : c + 1, :] = field[c, 0:1, :]
            x_out[1, c : c + 1, :] = field[c, rx - 1 : rx, :]
        halo = halo_recv_sem.at[par]
        remote(x_out.at[0], x_in.at[par, 1], halo_send_sem.at[0], halo.at[1], at(-1, 0)).start()
        remote(x_out.at[1], x_in.at[par, 0], halo_send_sem.at[1], halo.at[0], at(1, 0)).start()

        for t in range(tiles // 2):
            rows = pick(slice(t * 256, (t + 1) * 256), 256, field_b[...])
            for half in range(2):
                r = rows[:, half * 128 : (half + 1) * 128]
                x = jnp.where(
                    comp == 1, pltpu.roll(r, 32, 1), jnp.where(comp == 2, pltpu.roll(r, 64, 1), r)
                )
                for d in range(4):
                    y = x if d == 0 else pltpu.roll(x, 128 - 32 * d, 1)
                    z = jnp.where(here, y, 0.0)
                    m = jnp.concatenate(
                        [
                            jnp.sum(z[:4], axis=0, keepdims=True),
                            jnp.sum(z[4:], axis=0, keepdims=True),
                        ],
                        axis=0,
                    )
                    msg_out[(2 * t + half) * 4 + d] = m.astype(BF16)
        own = pltpu.make_async_copy(msg_out.at[me], msg_in.at[par, me], own_sem)
        own.start()
        for a, b in offsets:
            to = at(a, b)
            remote(
                msg_out.at[to["mx"] * n_my + to["my"]],
                msg_in.at[par, me],
                msg_send_sem,
                msg_recv_sem.at[par],
                to,
            ).start()

        y_out[...] = pick(edge_cols, 128, field_b[...]) + pick(edge_cols, 128, field_l[...])
        remote(y_out, y_in.at[par, 1], halo_send_sem.at[2], halo.at[3], at(0, -1)).start()
        remote(y_out, y_in.at[par, 0], halo_send_sem.at[3], halo.at[2], at(0, 1)).start()

        pl.when(step == 1)(tangents)

        for side in range(2):
            pltpu.make_async_copy(x_in.at[par, side], x_in.at[par, side], halo.at[side]).wait()
            pltpu.make_async_copy(y_in.at[par, side], y_in.at[par, side], halo.at[2 + side]).wait()
        own.wait()
        most = pl.ds(0, peers - 1)
        pltpu.make_async_copy(
            msg_in.at[par, most], msg_in.at[par, most], msg_recv_sem.at[par]
        ).wait()

        for t in range(tiles + 1):
            cols = slice(t * 128, (t + 1) * 128)
            if t < tiles:
                got = None
                for d in range(4):
                    m = msg_in[par, 4 * t + d].astype(F32)
                    u = jnp.concatenate(
                        [
                            jnp.broadcast_to(m[0:1], (4, 128)),
                            jnp.broadcast_to(m[1:2], (4, 128)),
                        ],
                        axis=0,
                    )
                    u = jnp.where(here, u, 0.0)
                    if d:
                        u = pltpu.roll(u, 32 * d, 1)
                    got = u if got is None else got + u
                got = jnp.where(
                    comp == 1,
                    pltpu.roll(got, 96, 1),
                    jnp.where(comp == 2, pltpu.roll(got, 64, 1), got),
                )
            else:
                got = jnp.where(
                    lane < rx, y_in[par, 1] * right_ok, y_in[par, 0] * left_ok
                )
            got = got * wrow[:, cols]
            scatter(got, t * 128, put_x[:, cols])
        scatter(got - got.astype(BF16).astype(F32), slots + 128, put_x[:, cols])
        coupled = jnp.dot(spread[...], put_y[...], preferred_element_type=F32)

        pltpu.make_async_copy(msg_out.at[most], msg_out.at[most], msg_send_sem).wait()
        for side in range(2):
            pltpu.make_async_copy(x_out.at[side], x_out.at[side], halo_send_sem.at[side]).wait()
            pltpu.make_async_copy(y_out, y_out, halo_send_sem.at[2 + side]).wait()

        st = stiff_s[...]

        def h(c):
            f = field[c]
            nb = across_x(
                f, x_in[par, 0, c : c + 1, :] * up_ok, x_in[par, 1, c : c + 1, :] * down_ok
            )
            nb += across_y(f, 0.0, 0.0)
            return rhs_ref[c] + st * nb + coupled[c * rx : (c + 1) * rx]

        update(h)
        return carry

    lax.fori_loop(1, ITERS, sweep, 0)

    sens = jnp.zeros((rx, ry), F32)
    for c in range(3):
        sens += field[c] * tangent[c] - field[c + 3] * tangent[c + 3]
    mine = -sens * dens_ref[...]
    sens_out[...] = mine
    sens_in[fr, :, :] = mine
    edge_out[0, :, :] = mine[:1, :128]
    edge_out[1, :, :] = mine[:1, ry - 128 :]
    edge_out[2, :, :] = mine[rx - 1 :, :128]
    edge_out[3, :, :] = mine[rx - 1 :, ry - 128 :]
    eye_l = onehot(sub_x, lane_row)
    eye_h = onehot(sub_x, lane_row - rx)
    edge_out[4, :, :] = jnp.sum(
        mine[:, :1] * eye_l + mine[:, ry - 1 :] * eye_h, axis=0, keepdims=True
    )
    routes = [
        (-1, 0, 0, 2, 2),
        (1, 0, 2, 0, 2),
        (0, -1, 4, 5, 1),
        (0, 1, 4, 4, 1),
        (-1, -1, 0, 6, 1),
        (-1, 1, 1, 7, 1),
        (1, -1, 2, 8, 1),
        (1, 1, 3, 9, 1),
    ]
    for df in range(n_freq):
        for a, b, src, dst, size in routes:
            remote(
                edge_out.at[pl.ds(src, size)],
                edge_in.at[fr, pl.ds(dst, size)],
                edge_send_sem,
                edge_recv_sem,
                at(a, b, df),
            ).start()
    for df in range(1, n_freq):
        remote(sens_out, sens_in.at[fr], sens_send_sem, sens_recv_sem, at(0, 0, df)).start()
    out_ref[...] = field[...]
    pltpu.make_async_copy(edge_in, edge_in, edge_recv_sem).wait()
    total_edge = [edge_in[0, k] for k in range(10)]
    for f in range(1, n_freq):
        total_edge = [total_edge[k] + edge_in[f, k] for k in range(10)]
    above = jnp.concatenate(total_edge[0:2], axis=1) * up_ok
    below = jnp.concatenate(total_edge[2:4], axis=1) * down_ok
    sides = jnp.where(low, total_edge[5] * right_ok, total_edge[4] * left_ok)
    down_right = total_edge[6][:, :1] * (down_ok * right_ok)
    down_left = total_edge[7][:, 127:] * (down_ok * left_ok)
    up_right = total_edge[8][:, :1] * (up_ok * right_ok)
    up_left = total_edge[9][:, 127:] * (up_ok * left_ok)
    before = jnp.where(
        lane_row == 0, up_right, jnp.where(lane_row == rx, up_left, pltpu.roll(sides, 1, 1))
    )
    after = jnp.where(
        lane_row == rx - 1,
        down_right,
        jnp.where(lane_row == 2 * rx - 1, down_left, pltpu.roll(sides, 127, 1)),
    )
    sides = sides + 0.5 * (before + after)
    col_right = jnp.sum(eye_l * sides, axis=1, keepdims=True)
    col_left = jnp.sum(eye_h * sides, axis=1, keepdims=True)
    others = pl.ds(0, n_freq - 1)
    pltpu.make_async_copy(sens_in.at[others], sens_in.at[others], sens_recv_sem).wait()
    total = sens_in[0]
    for f in range(1, n_freq):
        total += sens_in[f]
    total = total + 0.5 * across_x(total, above, below)
    total = total + 0.5 * across_y(total, col_left, col_right)
    filt_ref[...] = total / (4.0 * dens_ref[...])
    pltpu.make_async_copy(edge_in, edge_in, edge_send_sem).wait()
    pltpu.make_async_copy(sens_in.at[others], sens_in.at[others], sens_send_sem).wait()


def on_device(
    adjoint_rhs, state, density, stiffness, mass, omega, send_rows, recv_rows, mortar_weight
):
    rx, ry = density.shape
    slots = send_rows.shape[1]
    wide = slots + 128
    n_freq, n_mx, n_my = (lax.axis_size(name) for name in ("freq", "mx", "my"))
    peers = n_mx * n_my
    vmem = pl.BlockSpec(memory_space=pltpu.VMEM)
    field, filtered = pl.pallas_call(
        functools.partial(sweeps_kernel, n_freq, n_mx, n_my),
        out_shape=(
            jax.ShapeDtypeStruct((6, rx, ry), F32),
            jax.ShapeDtypeStruct((rx, ry), F32),
        ),
        in_specs=[vmem] * 5 + [pl.BlockSpec(memory_space=pltpu.SMEM)] + [vmem] * 3,
        out_specs=(vmem, vmem),
        scratch_shapes=[
            pltpu.VMEM((6, rx, ry), F32),
            pltpu.VMEM((6 * rx, ry), BF16),
            pltpu.VMEM((6 * rx, ry), BF16),
            pltpu.VMEM((rx, ry), F32),
            pltpu.VMEM((rx, ry), F32),
            pltpu.VMEM((rx, ry), F32),
            pltpu.VMEM((ry, wide), BF16),
            pltpu.VMEM((rx, wide), F32),
            pltpu.VMEM((wide + 128, ry), BF16),
            pltpu.VMEM((rx, wide), BF16),
            pltpu.VMEM((1, wide), F32),
            pltpu.VMEM((6 * rx, wide + 128), BF16),
            pltpu.VMEM((peers, 2, 128), BF16),
            pltpu.VMEM((2, peers, 2, 128), BF16),
            pltpu.VMEM((8, 128), F32),
            pltpu.VMEM((2, 2, 8, 128), F32),
            pltpu.VMEM((2, 8, ry), F32),
            pltpu.VMEM((2, 2, 8, ry), F32),
            pltpu.SemaphoreType.DMA,
            pltpu.SemaphoreType.DMA((2,)),
            pltpu.SemaphoreType.DMA,
            pltpu.SemaphoreType.DMA((4,)),
            pltpu.SemaphoreType.DMA((2, 4)),
            pltpu.VMEM((6, rx, ry), F32),
            pltpu.VMEM((2, 8, ry), F32),
            pltpu.VMEM((2, 8, ry), F32),
            pltpu.VMEM((8, 128), F32),
            pltpu.VMEM((2, 8, 128), F32),
            pltpu.SemaphoreType.DMA((4,)),
            pltpu.SemaphoreType.DMA((4,)),
            pltpu.VMEM((rx, ry), F32),
            pltpu.VMEM((n_freq, rx, ry), F32),
            pltpu.VMEM((5, 1, 128), F32),
            pltpu.VMEM((n_freq, 10, 1, 128), F32),
            pltpu.SemaphoreType.DMA,
            pltpu.SemaphoreType.DMA,
            pltpu.SemaphoreType.DMA,
            pltpu.SemaphoreType.DMA,
        ],
        compiler_params=pltpu.CompilerParams(collective_id=0, has_side_effects=True),
    )(
        adjoint_rhs.reshape(6, rx, ry),
        state.reshape(6, rx, ry),
        density,
        stiffness,
        mass,
        omega,
        send_rows,
        recv_rows,
        mortar_weight,
    )
    return field.reshape(1, 2, 3, rx, ry), filtered


def solution(mesh):
    return jax.shard_map(
        on_device,
        mesh=mesh,
        in_specs=(
            P("freq", None, None, "mx", "my"),
            P("freq", None, None, "mx", "my"),
            P("mx", "my"),
            P("mx", "my"),
            P("mx", "my"),
            P("freq"),
            P(("mx", "my"), None),
            P(("mx", "my"), None),
            P(("mx", "my"), None),
        ),
        out_specs=(P("freq", None, None, "mx", "my"), P("mx", "my")),
        check_vma=False,
    )
```

```python
import functools

import jax
import jax.numpy as jnp
from jax import lax
from jax.experimental import pallas as pl
from jax.experimental.pallas import tpu as pltpu
from jax.sharding import PartitionSpec as P

ITERS = 20
FAR = 3
MESH = pl.DeviceIdType.MESH
F32 = jnp.float32
BF16 = jnp.bfloat16


def onehot(a, b):
    return jnp.where(a == b, 1.0, 0.0).astype(F32)


def sweeps_kernel(
    n_freq,
    n_mx,
    n_my,
    rhs_ref,
    state_ref,
    dens_ref,
    stiffness_ref,
    mass_ref,
    omega_ref,
    send_ref,
    recv_ref,
    weight_ref,
    out_ref,
    filt_ref,
    field,
    field_b,
    field_l,
    stiff_s,
    gain_p,
    gain_q,
    pick_y,
    pick_x,
    put_y,
    put_x,
    wrow,
    spread,
    msg_out,
    msg_in,
    y_out,
    y_in,
    x_out,
    x_in,
    msg_send_sem,
    msg_recv_sem,
    own_sem,
    halo_send_sem,
    halo_recv_sem,
    tangent,
    sx_out,
    sx_in,
    sy_out,
    sy_in,
    state_send_sem,
    state_recv_sem,
    sens_out,
    sens_in,
    edge_out,
    edge_in,
    sens_send_sem,
    sens_recv_sem,
    edge_send_sem,
    edge_recv_sem,
    send_by,
    recv_by,
    weight_by,
    part,
):
    fr = lax.axis_index("freq")
    i = lax.axis_index("mx")
    j = lax.axis_index("my")
    peers = n_mx * n_my
    me = i * n_my + j
    rx, ry = dens_ref.shape
    slots = send_ref.shape[1]
    tiles = slots // 128

    def at(di, dj, df=0):
        return {
            "freq": lax.rem(fr + df, n_freq),
            "mx": lax.rem(i + di + n_mx, n_mx),
            "my": lax.rem(j + dj + n_my, n_my),
        }

    order_x = sorted(range(n_mx), key=lambda a: -min(a, n_mx - a))
    order_y = sorted(range(n_my), key=lambda b: -min(b, n_my - b))
    offsets = [(a, b) for b in order_y for a in order_x if a or b]

    barrier = pltpu.get_barrier_semaphore()
    for a, b in offsets:
        pl.semaphore_signal(barrier, inc=1, device_id=at(a, b), device_id_type=MESH)
    around = [(a, b) for a in (-1, 0, 1) for b in (-1, 0, 1)]
    for df in range(1, n_freq):
        for a, b in around:
            pl.semaphore_signal(barrier, inc=1, device_id=at(a, b, df), device_id_type=MESH)

    w = omega_ref[0]
    dens = dens_ref[...]
    mass = mass_ref[...]
    stiff = dens * dens * dens * stiffness_ref[...]
    rmass = dens * mass
    stiff_s[...] = stiff

    lane = lax.broadcasted_iota(jnp.int32, (8, 128), 1)
    sub = lax.broadcasted_iota(jnp.int32, (8, 128), 0)
    block = lax.shift_right_logical(lane, 5)
    comp = lax.bitwise_and(sub, 3)
    here = block == comp

    sub_y = lax.broadcasted_iota(jnp.int32, (ry, 128), 0)
    sub_x = lax.broadcasted_iota(jnp.int32, (rx, 128), 0)
    lane_y = lax.broadcasted_iota(jnp.int32, (128, ry), 1)
    lane_row = lax.broadcasted_iota(jnp.int32, (1, 128), 1)
    low = lane_row < rx

    def regroup(row_ref, to_ref):
        per = n_my // 4
        for g in range(n_mx // 4):
            parts = None
            for turn in range(4):
                picked = [
                    row_ref[:, pl.ds(((4 * g + (d + turn) % 4) * per + h) * 128, 128)]
                    for h in range(per)
                    for d in range(4)
                ]
                r = jnp.concatenate(picked, axis=0)
                if turn:
                    r = pltpu.roll(r, 32 * turn, 1)
                r = jnp.where(block == lax.bitwise_and(comp + turn, 3), r, jnp.zeros_like(r))
                parts = r if parts is None else parts + r
            for y in range(n_my):
                to_ref[y, :, g * 128 : (g + 1) * 128] = parts[y : y + 1]

    regroup(send_ref, send_by)
    regroup(recv_ref, recv_by)
    regroup(weight_ref, weight_by)
    run = n_mx * 32
    for n, b in enumerate(order_y):
        j_from = lax.rem(j - b + n_my, n_my)
        wrow[:, n * run : (n + 1) * run] = weight_by[j_from]
    for t in range(tiles + 1):
        cols = slice(t * 128, (t + 1) * 128)
        if t < tiles:
            n, g = divmod(t * 128, run)
            j_to = lax.rem(j + order_y[n], n_my)
            j_from = lax.rem(j - order_y[n] + n_my, n_my)
            src = send_by[j_to, :, g : g + 128]
            dst = recv_by[j_from, :, g : g + 128]
            sx, sy = lax.shift_right_logical(src, 8), lax.bitwise_and(src, ry - 1)
            dx, dy = lax.shift_right_logical(dst, 8), lax.bitwise_and(dst, ry - 1)
        else:
            sx = dx = jnp.where(low, lane_row, lane_row - rx)
            sy = jnp.where(low, 0, ry - 1)
            dy = jnp.where(low, ry - 1, 0)
        pick_y[:, cols] = onehot(sub_y, sy).astype(BF16)
        pick_x[:, cols] = onehot(sub_x, sx)
        put_x[:, cols] = onehot(sub_x, dx).astype(BF16)
        turned = jnp.broadcast_to(dy.astype(F32), (128, 128)).T.astype(jnp.int32)
        put_y[cols, :] = onehot(lane_y, jnp.concatenate([turned] * (ry // 128), axis=1)).astype(BF16)
    put_y[slots + 128 :, :] = put_y[slots : slots + 128, :]
    eye_low = onehot(sub_x, lane_row)
    eye_high = onehot(sub_x, lane_row - rx)
    wrow[:, slots:] = jnp.sum(
        stiff[:, ry - 1 :] * eye_low + stiff[:, :1] * eye_high, axis=0, keepdims=True
    )

    whole = wrow[:, :slots]
    hi = whole.astype(BF16)
    rest = whole - hi.astype(F32)
    mid = rest.astype(BF16)
    lo = (rest - mid.astype(F32)).astype(BF16)
    mdiag = jnp.zeros((rx, ry), F32)
    for piece in (hi, mid, lo):
        spread[0:rx, :slots] = put_x[:, :slots] * jnp.broadcast_to(piece, (rx, slots))
        mdiag += jnp.dot(spread[0:rx, :slots], put_y[:slots, :], preferred_element_type=F32)

    real_d = 4.4 * stiff + 0.3 + mdiag - w * w * rmass
    imag_d = 0.2 * w * (stiff + rmass)
    den = real_d * real_d + imag_d * imag_d
    gain_p[...] = real_d / den
    gain_q[...] = imag_d / den

    def update(h):
        p, q = gain_p[...], gain_q[...]
        for c in range(3):
            re, im = h(c), h(c + 3)
            new_re = re * p + im * q
            new_im = im * p - re * q
            for k, v in ((c, new_re), (c + 3, new_im)):
                field[k, :, :] = v
                high = v.astype(BF16)
                field_b[k * rx : (k + 1) * rx, :] = high
                field_l[k * rx : (k + 1) * rx, :] = (v - high.astype(F32)).astype(BF16)

    update(lambda c: rhs_ref[c])

    pl.semaphore_wait(barrier, peers - 1 + 9 * (n_freq - 1))

    up_ok = jnp.where(i > 0, 1.0, 0.0).astype(F32)
    down_ok = jnp.where(i < n_mx - 1, 1.0, 0.0).astype(F32)
    left_ok = jnp.where(j > 0, 1.0, 0.0).astype(F32)
    right_ok = jnp.where(j < n_my - 1, 1.0, 0.0).astype(F32)
    zero_row = jnp.zeros((1, 128), F32)

    def pick(cols, width, source):
        g = jnp.dot(source, pick_y[:, cols], preferred_element_type=F32)
        mask = pick_x[:, cols]
        rows = [
            jnp.sum(g[c * rx : (c + 1) * rx] * mask, axis=0, keepdims=True) for c in range(6)
        ]
        zero = jnp.zeros((1, width), F32)
        return jnp.concatenate(rows[:3] + [zero] + rows[3:] + [zero], axis=0)

    def remote(src, dst, ssem, rsem, to):
        return pltpu.make_async_remote_copy(
            src_ref=src, dst_ref=dst, send_sem=ssem, recv_sem=rsem, device_id=to, device_id_type=MESH
        )

    edge_cols = slice(slots, slots + 128)

    def scatter(got, start, mask):
        for c in range(6):
            r = c + c // 3
            spread[c * rx : (c + 1) * rx, start : start + 128] = mask * jnp.broadcast_to(
                got[r : r + 1].astype(BF16), (rx, 128)
            )

    lane_w = lax.broadcasted_iota(jnp.int32, (rx, ry), 1)
    sub_w = lax.broadcasted_iota(jnp.int32, (rx, ry), 0)

    def across_x(f, above, below):
        up = jnp.where(sub_w == 0, jnp.broadcast_to(above, (rx, ry)), pltpu.roll(f, 1, 0))
        down = jnp.where(
            sub_w == rx - 1, jnp.broadcast_to(below, (rx, ry)), pltpu.roll(f, rx - 1, 0)
        )
        return up + down

    def across_y(f, before, after):
        left = jnp.where(lane_w == 0, before, pltpu.roll(f, 1, 1))
        return left + jnp.where(lane_w == ry - 1, after, pltpu.roll(f, ry - 1, 1))

    for c in range(6):
        sx_out[0, c : c + 1, :] = state_ref[c, 0:1, :].astype(F32)
        sx_out[1, c : c + 1, :] = state_ref[c, rx - 1 : rx, :].astype(F32)
    sy_out[...] = pick(edge_cols, 128, state_ref[...].reshape(6 * rx, ry))
    state_copies = [
        remote(sx_out.at[0], sx_in.at[1], state_send_sem.at[0], state_recv_sem.at[1], at(-1, 0)),
        remote(sx_out.at[1], sx_in.at[0], state_send_sem.at[1], state_recv_sem.at[0], at(1, 0)),
        remote(sy_out, sy_in.at[1], state_send_sem.at[2], state_recv_sem.at[3], at(0, -1)),
        remote(sy_out, sy_in.at[0], state_send_sem.at[3], state_recv_sem.at[2], at(0, 1)),
    ]
    for copy in state_copies:
        copy.start()

    def tangents():
        for copy in state_copies:
            copy.wait()
        got = jnp.where(lane < rx, sy_in[1] * right_ok, sy_in[0] * left_ok)
        scatter(got, slots, put_x[:, edge_cols])
        sides = jnp.dot(spread[:, edge_cols], put_y[edge_cols, :], preferred_element_type=F32)
        d = dens_ref[...]
        dstiff = 3.0 * (d * d) * stiffness_ref[...]
        m = mass_ref[...]
        da = 4.4 * dstiff - w * w * m
        db = 0.2 * w * (dstiff + m)

        def beside(c):
            u = state_ref[c].astype(F32)
            nb = across_x(u, sx_in[0, c : c + 1, :] * up_ok, sx_in[1, c : c + 1, :] * down_ok)
            return u, nb + across_y(u, 0.0, 0.0) + sides[c * rx : (c + 1) * rx]

        for c in range(3):
            u_re, nb_re = beside(c)
            u_im, nb_im = beside(c + 3)
            tangent[c, :, :] = da * u_re - db * u_im - dstiff * nb_re
            tangent[c + 3, :, :] = da * u_im + db * u_re - dstiff * nb_im

    def sweep(step, carry):
        par = lax.rem(step, 2)

        halo = halo_recv_sem.at[par]

        own = pltpu.make_async_copy(
            msg_out.at[(n_my - 1) * n_mx + i], msg_in.at[par, n_my - 1, i], own_sem
        )
        for n, b in enumerate(order_y):
            if n == FAR:
                for c in range(6):
                    x_out[0, c : c + 1, :] = field[c, 0:1, :]
                    x_out[1, c : c + 1, :] = field[c, rx - 1 : rx, :]
                remote(x_out.at[0], x_in.at[par, 1], halo_send_sem.at[0], halo.at[1], at(-1, 0)).start()
                remote(x_out.at[1], x_in.at[par, 0], halo_send_sem.at[1], halo.at[0], at(1, 0)).start()

                y_out[...] = pick(edge_cols, 128, field_b[...]) + pick(edge_cols, 128, field_l[...])
                remote(y_out, y_in.at[par, 1], halo_send_sem.at[2], halo.at[3], at(0, -1)).start()
                remote(y_out, y_in.at[par, 0], halo_send_sem.at[3], halo.at[2], at(0, 1)).start()

            rows = pick(slice(n * run, (n + 1) * run), run, field_b[...])
            for half in range(n_mx // 4):
                r = rows[:, half * 128 : (half + 1) * 128]
                x = jnp.where(
                    comp == 1, pltpu.roll(r, 32, 1), jnp.where(comp == 2, pltpu.roll(r, 64, 1), r)
                )
                for d in range(4):
                    y = x if d == 0 else pltpu.roll(x, 128 - 32 * d, 1)
                    z = jnp.where(here, y, 0.0)
                    m = jnp.concatenate(
                        [
                            jnp.sum(z[:4], axis=0, keepdims=True),
                            jnp.sum(z[4:], axis=0, keepdims=True),
                        ],
                        axis=0,
                    )
                    msg_out[n * n_mx + half * 4 + d] = m.astype(BF16)
            for a in order_x:
                if a or b:
                    to = at(a, b)
                    remote(
                        msg_out.at[n * n_mx + to["mx"]],
                        msg_in.at[par, n, i],
                        msg_send_sem,
                        msg_recv_sem.at[par, n],
                        to,
                    ).start()
                else:
                    own.start()

        pl.when(step == 1)(tangents)

        def arrived(n):
            if order_y[n]:
                group = msg_in.at[par, n]
            else:
                own.wait()
                group = msg_in.at[par, n, pl.ds(0, n_mx - 1)]
            pltpu.make_async_copy(group, group, msg_recv_sem.at[par, n]).wait()
            for half in range(n_mx // 4):
                got = None
                for d in range(4):
                    m = msg_in[par, n, 4 * half + d].astype(F32)
                    u = jnp.concatenate(
                        [
                            jnp.broadcast_to(m[0:1], (4, 128)),
                            jnp.broadcast_to(m[1:2], (4, 128)),
                        ],
                        axis=0,
                    )
                    u = jnp.where(here, u, 0.0)
                    if d:
                        u = pltpu.roll(u, 32 * d, 1)
                    got = u if got is None else got + u
                got = jnp.where(
                    comp == 1,
                    pltpu.roll(got, 96, 1),
                    jnp.where(comp == 2, pltpu.roll(got, 64, 1), got),
                )
                start = n * run + half * 128
                cols = slice(start, start + 128)
                scatter(got * wrow[:, cols], start, put_x[:, cols])

        for side in range(2):
            pltpu.make_async_copy(x_in.at[par, side], x_in.at[par, side], halo.at[side]).wait()
            pltpu.make_async_copy(y_in.at[par, side], y_in.at[par, side], halo.at[2 + side]).wait()
        got = jnp.where(lane < rx, y_in[par, 1] * right_ok, y_in[par, 0] * left_ok)
        got = got * wrow[:, edge_cols]
        scatter(got, slots, put_x[:, edge_cols])
        scatter(got - got.astype(BF16).astype(F32), slots + 128, put_x[:, edge_cols])
        for n in range(n_my - 1, FAR - 1, -1):
            arrived(n)
        near = jnp.dot(
            spread[:, FAR * run :], put_y[FAR * run :, :], preferred_element_type=F32
        )
        st = stiff_s[...]
        for c in range(6):
            f = field[c]
            nb = across_x(
                f, x_in[par, 0, c : c + 1, :] * up_ok, x_in[par, 1, c : c + 1, :] * down_ok
            )
            nb += across_y(f, 0.0, 0.0)
            part[c, :, :] = rhs_ref[c] + st * nb + near[c * rx : (c + 1) * rx]

        most = pl.ds(0, peers - 1)
        pltpu.make_async_copy(msg_out.at[most], msg_out.at[most], msg_send_sem).wait()
        for side in range(2):
            pltpu.make_async_copy(x_out.at[side], x_out.at[side], halo_send_sem.at[side]).wait()
            pltpu.make_async_copy(y_out, y_out, halo_send_sem.at[2 + side]).wait()

        for n in range(FAR - 1, -1, -1):
            arrived(n)
        distant = jnp.dot(
            spread[:, : FAR * run], put_y[: FAR * run, :], preferred_element_type=F32
        )
        update(lambda c: part[c] + distant[c * rx : (c + 1) * rx])
        return carry

    lax.fori_loop(1, ITERS, sweep, 0)

    sens = jnp.zeros((rx, ry), F32)
    for c in range(3):
        sens += field[c] * tangent[c] - field[c + 3] * tangent[c + 3]
    mine = -sens * dens_ref[...]
    sens_out[...] = mine
    sens_in[fr, :, :] = mine
    edge_out[0, :, :] = mine[:1, :128]
    edge_out[1, :, :] = mine[:1, ry - 128 :]
    edge_out[2, :, :] = mine[rx - 1 :, :128]
    edge_out[3, :, :] = mine[rx - 1 :, ry - 128 :]
    eye_l = onehot(sub_x, lane_row)
    eye_h = onehot(sub_x, lane_row - rx)
    edge_out[4, :, :] = jnp.sum(
        mine[:, :1] * eye_l + mine[:, ry - 1 :] * eye_h, axis=0, keepdims=True
    )
    routes = [
        (-1, 0, 0, 2, 2),
        (1, 0, 2, 0, 2),
        (0, -1, 4, 5, 1),
        (0, 1, 4, 4, 1),
        (-1, -1, 0, 6, 1),
        (-1, 1, 1, 7, 1),
        (1, -1, 2, 8, 1),
        (1, 1, 3, 9, 1),
    ]
    for df in range(n_freq):
        for a, b, src, dst, size in routes:
            remote(
                edge_out.at[pl.ds(src, size)],
                edge_in.at[fr, pl.ds(dst, size)],
                edge_send_sem,
                edge_recv_sem,
                at(a, b, df),
            ).start()
    for df in range(1, n_freq):
        remote(sens_out, sens_in.at[fr], sens_send_sem, sens_recv_sem, at(0, 0, df)).start()
    out_ref[...] = field[...]
    pltpu.make_async_copy(edge_in, edge_in, edge_recv_sem).wait()
    total_edge = [edge_in[0, k] for k in range(10)]
    for f in range(1, n_freq):
        total_edge = [total_edge[k] + edge_in[f, k] for k in range(10)]
    above = jnp.concatenate(total_edge[0:2], axis=1) * up_ok
    below = jnp.concatenate(total_edge[2:4], axis=1) * down_ok
    sides = jnp.where(low, total_edge[5] * right_ok, total_edge[4] * left_ok)
    down_right = total_edge[6][:, :1] * (down_ok * right_ok)
    down_left = total_edge[7][:, 127:] * (down_ok * left_ok)
    up_right = total_edge[8][:, :1] * (up_ok * right_ok)
    up_left = total_edge[9][:, 127:] * (up_ok * left_ok)
    before = jnp.where(
        lane_row == 0, up_right, jnp.where(lane_row == rx, up_left, pltpu.roll(sides, 1, 1))
    )
    after = jnp.where(
        lane_row == rx - 1,
        down_right,
        jnp.where(lane_row == 2 * rx - 1, down_left, pltpu.roll(sides, 127, 1)),
    )
    sides = sides + 0.5 * (before + after)
    col_right = jnp.sum(eye_l * sides, axis=1, keepdims=True)
    col_left = jnp.sum(eye_h * sides, axis=1, keepdims=True)
    others = pl.ds(0, n_freq - 1)
    pltpu.make_async_copy(sens_in.at[others], sens_in.at[others], sens_recv_sem).wait()
    total = sens_in[0]
    for f in range(1, n_freq):
        total += sens_in[f]
    total = total + 0.5 * across_x(total, above, below)
    total = total + 0.5 * across_y(total, col_left, col_right)
    filt_ref[...] = total / (4.0 * dens_ref[...])
    pltpu.make_async_copy(edge_in, edge_in, edge_send_sem).wait()
    pltpu.make_async_copy(sens_in.at[others], sens_in.at[others], sens_send_sem).wait()


def on_device(
    adjoint_rhs, state, density, stiffness, mass, omega, send_rows, recv_rows, mortar_weight
):
    rx, ry = density.shape
    slots = send_rows.shape[1]
    wide = slots + 128
    n_freq, n_mx, n_my = (lax.axis_size(name) for name in ("freq", "mx", "my"))
    peers = n_mx * n_my
    vmem = pl.BlockSpec(memory_space=pltpu.VMEM)
    field, filtered = pl.pallas_call(
        functools.partial(sweeps_kernel, n_freq, n_mx, n_my),
        out_shape=(
            jax.ShapeDtypeStruct((6, rx, ry), F32),
            jax.ShapeDtypeStruct((rx, ry), F32),
        ),
        in_specs=[vmem] * 5 + [pl.BlockSpec(memory_space=pltpu.SMEM)] + [vmem] * 3,
        out_specs=(vmem, vmem),
        scratch_shapes=[
            pltpu.VMEM((6, rx, ry), F32),
            pltpu.VMEM((6 * rx, ry), BF16),
            pltpu.VMEM((6 * rx, ry), BF16),
            pltpu.VMEM((rx, ry), F32),
            pltpu.VMEM((rx, ry), F32),
            pltpu.VMEM((rx, ry), F32),
            pltpu.VMEM((ry, wide), BF16),
            pltpu.VMEM((rx, wide), F32),
            pltpu.VMEM((wide + 128, ry), BF16),
            pltpu.VMEM((rx, wide), BF16),
            pltpu.VMEM((1, wide), F32),
            pltpu.VMEM((6 * rx, wide + 128), BF16),
            pltpu.VMEM((peers, 2, 128), BF16),
            pltpu.VMEM((2, n_my, n_mx, 2, 128), BF16),
            pltpu.VMEM((8, 128), F32),
            pltpu.VMEM((2, 2, 8, 128), F32),
            pltpu.VMEM((2, 8, ry), F32),
            pltpu.VMEM((2, 2, 8, ry), F32),
            pltpu.SemaphoreType.DMA,
            pltpu.SemaphoreType.DMA((2, n_my)),
            pltpu.SemaphoreType.DMA,
            pltpu.SemaphoreType.DMA((4,)),
            pltpu.SemaphoreType.DMA((2, 4)),
            pltpu.VMEM((6, rx, ry), F32),
            pltpu.VMEM((2, 8, ry), F32),
            pltpu.VMEM((2, 8, ry), F32),
            pltpu.VMEM((8, 128), F32),
            pltpu.VMEM((2, 8, 128), F32),
            pltpu.SemaphoreType.DMA((4,)),
            pltpu.SemaphoreType.DMA((4,)),
            pltpu.VMEM((rx, ry), F32),
            pltpu.VMEM((n_freq, rx, ry), F32),
            pltpu.VMEM((5, 1, 128), F32),
            pltpu.VMEM((n_freq, 10, 1, 128), F32),
            pltpu.SemaphoreType.DMA,
            pltpu.SemaphoreType.DMA,
            pltpu.SemaphoreType.DMA,
            pltpu.SemaphoreType.DMA,
            pltpu.VMEM((n_my, 1, n_mx * 32), jnp.int32),
            pltpu.VMEM((n_my, 1, n_mx * 32), jnp.int32),
            pltpu.VMEM((n_my, 1, n_mx * 32), F32),
            pltpu.VMEM((6, rx, ry), F32),
        ],
        compiler_params=pltpu.CompilerParams(collective_id=0, has_side_effects=True),
    )(
        adjoint_rhs.reshape(6, rx, ry),
        state.reshape(6, rx, ry),
        density,
        stiffness,
        mass,
        omega,
        send_rows,
        recv_rows,
        mortar_weight,
    )
    return field.reshape(1, 2, 3, rx, ry), filtered


def solution(mesh):
    return jax.shard_map(
        on_device,
        mesh=mesh,
        in_specs=(
            P("freq", None, None, "mx", "my"),
            P("freq", None, None, "mx", "my"),
            P("mx", "my"),
            P("mx", "my"),
            P("mx", "my"),
            P("freq"),
            P(("mx", "my"), None),
            P(("mx", "my"), None),
            P(("mx", "my"), None),
        ),
        out_specs=(P("freq", None, None, "mx", "my"), P("mx", "my")),
        check_vma=False,
    )
```
